32 devices in a mesh: tok: 4 (over y, core), ch: 8 (over z, x).
Axes of the slice: x: 2, y: 2, z: 4, core: 2. Of those that a mesh axis runs over, the one named last changes fastest.
Arguments:
- tokens: bfloat16 [4096, 4096], P('tok', 'ch'), may hold values from -6 to 6
- w_in: bfloat16 [4096, 16384], P('tok', 'ch'), may hold values from -0.09375 to 0.09375
- b_in: float32 [16384], P('ch'), may hold values from -3 to 3
- dw_kernel: float32 [9, 16384], P(None, 'ch'), may hold values from -2 to 2
- dw_bias: float32 [16384], P('ch'), may hold values from -3 to 3
- w_out: bfloat16 [16384, 4096], P('ch', 'tok'), may hold values from -0.0625 to 0.0625
- b_out: float32 [4096], P('ch'), may hold values from -3 to 3
Outputs:
- mixed: bfloat16 [4096, 4096], P('tok', 'ch')
The draws below stay inside these ranges and needn't reach their ends.
All inputs are finite; a program needn't handle non-finite values.
Results may differ from the reference program's by a relative error of at most 0.0055.
Values may be sent and summed in bfloat16 or wider, within the bound.
No kernel may reach another device: no remote copies, remote signals or barrier semaphores. Data moves between devices by JAX's collectives and lax.ppermute only.
A program may use at most 128 MiB of HBM per device.

```python
import math
import jax
import jax.numpy as jnp
from jax import lax

D = 4096
FF = 16384
IMAGES = 2
GRIDW = 64
TOKENS = 4096


def strengthened(entries, stream_key, source, target, blocks, factor):
    def block_of(dim):
        return (jnp.arange(entries.shape[dim]) // (entries.shape[dim] // blocks)).reshape((-1,) + (1,) * (entries.ndim - 1 - dim))

    first = jax.random.permutation(stream_key, blocks)[block_of(target)]
    second = (block_of(target) + blocks // 2) % blocks
    return jnp.where((block_of(source) == first) | (block_of(source) == second), factor * entries, entries)


def block_scale(rng, extent, cuts, low, top_value):
    level, own = 1.0, jax.random.fold_in(rng, 6)
    for position, parts in cuts:
        steps = jnp.exp(jax.random.uniform(jax.random.fold_in(own, position), (parts,), jnp.float32, low / len(cuts), top_value / len(cuts)))
        level = level * jnp.repeat(steps, extent[position] // parts).reshape([-1 if axis == position else 1 for axis in range(len(extent))])
    return level


def bell_draw(rng, dims, scale, bound, shards=(), held_as=jnp.bfloat16):
    drawn = scale * jax.random.normal(rng, dims, jnp.float32)
    if shards:
        drawn = drawn * block_scale(rng, dims, shards, -0.22, 0.18)
    return jnp.clip(drawn, -bound, bound).astype(held_as)


def bell_draw_with(key, dims, spread, limit, pieces, heavy, held_as=jnp.bfloat16):
    drawn = spread * jax.random.normal(key, dims, jnp.float32)
    if pieces:
        drawn = drawn * block_scale(key, dims, pieces, -0.22, 0.18)
    return jnp.clip(strengthened(drawn, jax.random.fold_in(key, 3), *heavy), -limit, limit).astype(held_as)


def setup_inputs(seed: int = 0) -> dict:
    streams_of = jax.random.split(jax.random.key(seed), 8)
    tokens = bell_draw(streams_of[0], (TOKENS, D), 1.0, 6.0, ((0, 4), (1, 8)))
    w_in = bell_draw(streams_of[1], (D, FF), D ** -0.5, 0.09375, ((0, 4), (1, 8)))
    b_in = bell_draw(streams_of[2], (FF,), 0.5, 3.0, ((0, 8),), jnp.float32)
    dw_kernel = bell_draw(streams_of[3], (9, FF), 0.35, 2.0, ((1, 8),), jnp.float32)
    dw_bias = bell_draw(streams_of[4], (FF,), 0.5, 3.0, ((0, 8),), jnp.float32)
    w_out = bell_draw_with(streams_of[5], (FF, D), FF ** -0.5, 0.0625, ((0, 8), (1, 4)), (0, 1, 8, 2.0))
    b_out = bell_draw(streams_of[6], (D,), 0.5, 3.0, ((0, 8),), jnp.float32)
    return dict(tokens=tokens, w_in=w_in, b_in=b_in, dw_kernel=dw_kernel, dw_bias=dw_bias, w_out=w_out, b_out=b_out)


def reference(tokens, w_in, b_in, dw_kernel, dw_bias, w_out, b_out):
    height = TOKENS // (IMAGES * GRIDW)
    block = math.gcd(FF, 2048)
    count = FF // block

    def one_block(total, index):
        start = (index * block).astype(jnp.int32)
        w_piece = lax.dynamic_slice_in_dim(w_in, start, block, 1)
        bias_piece = lax.dynamic_slice_in_dim(b_in, start, block, 0)
        pre = (jnp.dot(tokens, w_piece, preferred_element_type=jnp.float32) + bias_piece).astype(jnp.bfloat16)
        grid = pre.reshape(height, IMAGES, GRIDW, block).astype(jnp.float32)
        padded = jnp.pad(grid, ((1, 1), (0, 0), (1, 1), (0, 0)))
        taps = lax.dynamic_slice_in_dim(dw_kernel, start, block, 1).astype(jnp.float32)
        conv = lax.dynamic_slice_in_dim(dw_bias, start, block, 0).astype(jnp.float32) + jnp.zeros_like(grid)
        for row_off in range(3):
            for col_off in range(3):
                conv = conv + taps[3 * row_off + col_off] * padded[row_off:row_off + height, :, col_off:col_off + GRIDW, :]
        act = jax.nn.gelu(conv, approximate=False).astype(jnp.bfloat16).reshape(TOKENS, block)
        rows_out = lax.dynamic_slice_in_dim(w_out, start, block, 0)
        return total + jnp.dot(act, rows_out, preferred_element_type=jnp.float32), None

    total, _ = lax.scan(one_block, jnp.zeros((TOKENS, D), jnp.float32), jnp.arange(count, dtype=jnp.int32))
    return (total + b_out).astype(jnp.bfloat16)
```

```python
import functools

import jax
import jax.numpy as jnp
from jax import lax
from jax.experimental import pallas as pl
from jax.experimental.pallas import tpu as pltpu
from jax.sharding import PartitionSpec as P

IMAGES = 2
GRIDW = 64
BAND = IMAGES * GRIDW
CORES = 2
LANES = 128
HALVES = 2
LAST_SPLITS = 2
CONV_TILE = 512


def blank(*shape):
    return pl.pallas_call(
        lambda ref: None,
        out_shape=jax.ShapeDtypeStruct(shape, jnp.bfloat16),
        out_specs=pl.BlockSpec(memory_space=pl.ANY),
    )()


def conv_kernel(halves, *refs):
    pre_refs = refs[:halves]
    before_ref, after_ref, taps_ref, bias_ref, out_ref, left, right = refs[halves:]
    rows, tile = out_ref.shape
    height = rows // BAND
    per = pl.num_programs(0) // halves

    def run(pre_ref):
        def body(n, _):
            lanes = pl.ds(pl.multiple_of(n // IMAGES * LANES, LANES), LANES)
            first = n % IMAGES * GRIDW
            taps = [taps_ref[i:i + 1, lanes] for i in range(9)]
            bias = bias_ref[:, lanes]
            left[7:8] = jnp.zeros((1, LANES), jnp.float32)
            right[GRIDW:GRIDW + 1] = jnp.zeros((1, LANES), jnp.float32)

            def row(h):
                ref, base = pre_ref, h * BAND
                if h < 0:
                    ref, base = before_ref, 0
                if h >= height:
                    ref, base = after_ref, 0
                at = pl.ds(pl.multiple_of(first + base, GRIDW), GRIDW)
                return at, ref[at, lanes].astype(jnp.float32)

            above, here = row(-1)[1], row(0)[1]
            for h in range(height):
                below = row(h + 1)[1]
                left[8:8 + GRIDW] = above * taps[0] + here * taps[3] + below * taps[6]
                right[0:GRIDW] = above * taps[2] + here * taps[5] + below * taps[8]
                conv = bias + (above * taps[1] + here * taps[4] + below * taps[7])
                conv = conv + left[7:7 + GRIDW] + right[1:1 + GRIDW]
                act = 0.5 * conv * (1.0 + lax.erf(conv * 0.5 ** 0.5))
                at = pl.ds(pl.multiple_of(first + h * BAND, GRIDW), GRIDW)
                out_ref[at, lanes] = act.astype(out_ref.dtype)
                above, here = here, below
            return 0

        lax.fori_loop(0, IMAGES * (tile // LANES), body, 0)

    for f in range(halves):
        pl.when(pl.program_id(0) // per == f)(functools.partial(run, pre_refs[f]))


def convolve(pres, before, after, taps, bias):
    rows, part = pres[0].shape
    halves = len(pres)
    tile = min(CONV_TILE, part)
    per = part // tile

    def pre_map(f):
        return lambda i: (0, jnp.clip(i - f * per, 0, per - 1))

    def wide(n):
        return pl.BlockSpec((n, tile), lambda i: (0, i))

    return pl.pallas_call(
        functools.partial(conv_kernel, halves),
        grid=(halves * per,),
        in_specs=[pl.BlockSpec((rows, tile), pre_map(f)) for f in range(halves)]
        + [wide(BAND), wide(BAND), wide(9), wide(1)],
        out_specs=wide(rows),
        out_shape=jax.ShapeDtypeStruct((rows, halves * part), jnp.bfloat16),
        scratch_shapes=[pltpu.VMEM((GRIDW + 16, LANES), jnp.float32)] * 2,
        compiler_params=pltpu.CompilerParams(vmem_limit_bytes=24 << 20),
        cost_estimate=pl.CostEstimate(flops=60 * rows * halves * part, bytes_accessed=4 * rows * halves * part, transcendentals=0),
    )(*pres, before, after, taps, bias[None])


def local(tokens, w_in, b_in, dw_kernel, dw_bias, w_out, b_out):
    nt, nc = lax.axis_size("tok"), lax.axis_size("ch")
    nz, nx, ny = nt, nc // nt, nt // CORES
    t, c = lax.axis_index("tok"), lax.axis_index("ch")
    z, x = c // nx, c % nx
    y, core = t // CORES, t % CORES
    rows, width = tokens.shape
    depth, hidden = w_in.shape
    part = hidden // HALVES

    def zshift(k):
        return [(i, (i + k * nx) % nc) for i in range(nc)]

    def xshift(k):
        return [(i, i // nx * nx + (i + k) % nx) for i in range(nc)]

    def yshift(k):
        return [(i, (i + CORES * k) % nt) for i in range(nt)]

    swap = [(i, i ^ 1) for i in range(nt)]

    def owner(k, other):
        return (y + ny - k) % ny * CORES + (1 - core if other else core)

    held = tokens
    span = nx * width
    early = (nz - 1) * span
    whole = blank(rows, early)
    last = blank(rows, span)
    for s in range(nz):
        if s:
            held = lax.ppermute(held, "ch", zshift(1))
        for k in range(nx):
            block = lax.ppermute(held, "ch", xshift(k)) if k else held
            start = (x + nx - k) % nx * width
            if s < nz - 1:
                whole = lax.dynamic_update_slice_in_dim(whole, block, s * span + start, 1)
            else:
                last = lax.dynamic_update_slice_in_dim(last, block, start, 1)

    partner = lax.ppermute(w_in, "tok", swap)
    pres = []
    for f in range(HALVES):
        cut = slice(f * part, (f + 1) * part)
        stack = blank(nz * depth, part)
        for k in range(ny):
            mine = lax.ppermute(w_in[:, cut], "tok", yshift(k)) if k else w_in[:, cut]
            pair = lax.ppermute(mine, "tok", swap) if k else partner[:, cut]
            for other, block in ((0, mine), (1, pair)):
                stack = lax.dynamic_update_slice_in_dim(stack, block, (z + nz - owner(k, other)) % nz * depth, 0)
        total = jnp.dot(whole, stack[:early], preferred_element_type=jnp.float32)
        total = total + jnp.dot(last, stack[early:], preferred_element_type=jnp.float32)
        pres.append((total + b_in[cut]).astype(jnp.bfloat16))

    up = [(i, i + 1) for i in range(nt - 1)]
    down = [(i + 1, i) for i in range(nt - 1)]
    before = lax.ppermute(jnp.concatenate([p[-BAND:] for p in pres], axis=1), "tok", up)
    after = lax.ppermute(jnp.concatenate([p[:BAND] for p in pres], axis=1), "tok", down)
    act = convolve(pres, before, after, dw_kernel, dw_bias)

    pieces = max(1, width // LANES)
    cols = width // pieces
    outs = []
    for q in range(pieces):
        piece = jnp.concatenate(
            [lax.dynamic_slice_in_dim(w_out, (x + k) % nx * width + q * cols, cols, 1) for k in range(nx)], axis=1
        )
        blocks = []
        for k in range(ny):
            mine = lax.ppermute(piece, "tok", yshift(k)) if k else piece
            blocks += [mine, lax.ppermute(mine, "tok", swap)]
        dots = [jnp.dot(act, b, preferred_element_type=jnp.float32) for b in blocks]
        base = jnp.concatenate([d[:, :cols] for d in dots], axis=1)
        splits = LAST_SPLITS if q == pieces - 1 else 1
        step = rows // splits
        bands = []
        for h in range(splits):
            cut = slice(h * step, (h + 1) * step)
            total = base[cut]
            if h:
                total, _ = lax.optimization_barrier((total, done))
            for k in range(1, nx):
                share = jnp.concatenate([d[cut, k * cols:(k + 1) * cols].astype(jnp.bfloat16) for d in dots], axis=1)
                other = lax.ppermute(share, "ch", xshift(k))
                total = total + other.astype(jnp.float32)

            def term(s):
                goal = (z + nz - s) % nz
                place = (y + ny - goal // CORES) % ny * CORES + (goal + core) % CORES
                return lax.dynamic_slice_in_dim(total, place * cols, cols, 1)

            done = term(0)
            for s in range(1, nz):
                done = done + lax.ppermute(term(s).astype(jnp.bfloat16), "ch", zshift(nz - s)).astype(jnp.float32)
            bands.append(done)
        outs.append(jnp.concatenate(bands, axis=0))
    return (jnp.concatenate(outs, axis=1) + b_out).astype(jnp.bfloat16)


def solution(mesh):
    in_specs = (
        P("tok", "ch"),
        P("tok", "ch"),
        P("ch"),
        P(None, "ch"),
        P("ch"),
        P("ch", "tok"),
        P("ch"),
    )
    return jax.shard_map(local, mesh=mesh, in_specs=in_specs, out_specs=P("tok", "ch"), check_vma=False)
```

```python
import functools

import jax
import jax.numpy as jnp
from jax import lax
from jax.experimental import pallas as pl
from jax.experimental.pallas import tpu as pltpu
from jax.sharding import PartitionSpec as P

IMAGES = 2
GRIDW = 64
BAND = IMAGES * GRIDW
CORES = 2
LANES = 128
TILES = 4
SPLITS = 2
MM_VMEM = 60 << 20
MM_ROWS = 512


def mm_kernel(places, homes, base, start_ref, bias_ref, *refs):
    many = max(i for tile_homes in homes for i, _ in tile_homes) + 1
    toks, weights = refs[:len(places)], refs[len(places):len(places) + many]
    out, first, final, tok, held, stage, acc, tsem, wsem, osem = refs[-10:]
    nz, rows, _ = tok.shape
    _, tile = held.shape[2:]
    nx = start_ref.shape[0] - nz

    def tok_copy(i):
        row, s, k = places[i]
        n, width = toks[i].shape
        col = pl.multiple_of(start_ref[k], width)
        return pltpu.make_async_copy(toks[i], tok.at[s, pl.ds(row, n), pl.ds(col, width)], tsem.at[i])

    def weight_copy(t, r):
        ref, col = homes[t][r]
        slot = start_ref[nx + r]
        return pltpu.make_async_copy(weights[ref].at[:, pl.ds(col, tile)], held.at[t % 2, slot], wsem.at[t % 2, slot])

    def weight_wait(t, s):
        pltpu.make_async_copy(weights[0].at[:, pl.ds(0, tile)], held.at[t % 2, s], wsem.at[t % 2, s]).wait()

    def out_copies(t):
        cols = pl.ds(t * tile, tile)
        kept = stage.at[t % 2]
        return [
            pltpu.make_async_copy(kept, out.at[:, pl.ds((base + t) * tile, tile)], osem.at[t % 2, 0]),
            pltpu.make_async_copy(kept.at[pl.ds(0, BAND)], first.at[:, cols], osem.at[t % 2, 1]),
            pltpu.make_async_copy(kept.at[pl.ds(rows - BAND, BAND)], final.at[:, cols], osem.at[t % 2, 2]),
        ]

    tiles = len(homes)
    step = min(MM_ROWS, rows)
    by_slot = [[i for i in range(len(places)) if places[i][1] == s] for s in range(nz)]
    for i in by_slot[0]:
        tok_copy(i).start()
    for r in range(nz):
        weight_copy(0, r).start()
    for s in range(1, nz):
        for i in by_slot[s]:
            tok_copy(i).start()
    for t in range(tiles):
        if t + 1 < tiles:
            for r in range(nz):
                weight_copy(t + 1, r).start()
        if t >= 2:
            for copy in out_copies(t - 2):
                copy.wait()
        for group in ([[s] for s in range(nz)] if t == 0 else [list(range(nz))]):
            for s in group:
                if t == 0:
                    for i in by_slot[s]:
                        tok_copy(i).wait()
                weight_wait(t, s)

            def body(m, _, group=group, t=t):
                at = pl.ds(pl.multiple_of(m * step, step), step)
                if group[0] == 0:
                    total = bias_ref[:, (base + t) * tile:(base + t + 1) * tile] + jnp.zeros((step, tile), jnp.float32)
                else:
                    total = acc[at, :]
                for s in group:
                    total = total + jnp.dot(tok[s, at, :], held[t % 2, s], preferred_element_type=jnp.float32)
                if group[-1] == nz - 1:
                    stage[t % 2, at, :] = total.astype(stage.dtype)
                else:
                    acc[at, :] = total
                return 0

            lax.fori_loop(0, rows // step, body, 0)
        for copy in out_copies(t):
            copy.start()
    for t in range(max(0, tiles - 2), tiles):
        for copy in out_copies(t):
            copy.wait()


def project(starts, bias, toks, places, weights, homes, base, old, rows, depth, tile, nz):
    part = tile * len(homes)
    anywhere = pl.BlockSpec(memory_space=pl.ANY)
    return pl.pallas_call(
        functools.partial(mm_kernel, places, homes, base),
        in_specs=[pl.BlockSpec(memory_space=pltpu.SMEM), pl.BlockSpec(memory_space=pltpu.VMEM)]
        + [anywhere] * (len(toks) + len(weights) + len(old)),
        out_specs=[anywhere] * 3,
        out_shape=[jax.ShapeDtypeStruct(dims, jnp.bfloat16) for dims in ((rows, bias.shape[0]), (BAND, part), (BAND, part))],
        input_output_aliases={2 + len(toks) + len(weights) + i: i for i in range(len(old))},
        scratch_shapes=[
            pltpu.VMEM((nz, rows, depth), jnp.bfloat16),
            pltpu.VMEM((2, nz, depth, tile), jnp.bfloat16),
            pltpu.VMEM((2, rows, tile), jnp.bfloat16),
            pltpu.VMEM((rows, tile), jnp.float32),
            pltpu.SemaphoreType.DMA((len(toks),)),
            pltpu.SemaphoreType.DMA((2, nz)),
            pltpu.SemaphoreType.DMA((2, 3)),
        ],
        compiler_params=pltpu.CompilerParams(vmem_limit_bytes=MM_VMEM),
        cost_estimate=pl.CostEstimate(flops=2 * rows * nz * depth * part, bytes_accessed=2 * nz * depth * (rows + part), transcendentals=0),
    )(starts, bias[None], *toks, *weights, *old)


def conv_kernel(parts, pre_ref, *refs):
    n = len(parts)
    taps_ref, bias_ref, out_ref, left, right = refs[2 * n:]
    for f, (lo, hi) in enumerate(parts):
        inside = (pl.program_id(0) >= lo) & (pl.program_id(0) < hi)
        pl.when(inside)(functools.partial(conv_tile, pre_ref, refs[f], refs[n + f], taps_ref, bias_ref, out_ref, left, right))


def conv_tile(pre_ref, before_ref, after_ref, taps_ref, bias_ref, out_ref, left, right):
    rows, tile = out_ref.shape
    height = rows // BAND

    def body(n, _):
        lanes = pl.ds(pl.multiple_of(n // IMAGES * LANES, LANES), LANES)
        first = n % IMAGES * GRIDW
        taps = [taps_ref[i:i + 1, lanes] for i in range(9)]
        bias = bias_ref[:, lanes]
        left[7:8] = jnp.zeros((1, LANES), jnp.float32)
        right[GRIDW:GRIDW + 1] = jnp.zeros((1, LANES), jnp.float32)

        def row(h):
            ref, base = pre_ref, h * BAND
            if h < 0:
                ref, base = before_ref, 0
            if h >= height:
                ref, base = after_ref, 0
            at = pl.ds(pl.multiple_of(first + base, GRIDW), GRIDW)
            return ref[at, lanes].astype(jnp.float32)

        above, here = row(-1), row(0)
        for h in range(height):
            below = row(h + 1)
            left[8:8 + GRIDW] = above * taps[0] + here * taps[3] + below * taps[6]
            right[0:GRIDW] = above * taps[2] + here * taps[5] + below * taps[8]
            conv = bias + (above * taps[1] + here * taps[4] + below * taps[7])
            conv = conv + left[7:7 + GRIDW] + right[1:1 + GRIDW]
            act = 0.5 * conv * (1.0 + lax.erf(conv * 0.5 ** 0.5))
            at = pl.ds(pl.multiple_of(first + h * BAND, GRIDW), GRIDW)
            out_ref[at, lanes] = act.astype(out_ref.dtype)
            above, here = here, below
        return 0

    lax.fori_loop(0, IMAGES * (tile // LANES), body, 0)


def convolve(pre, befores, afters, taps, bias, tile, parts):
    rows, hidden = pre.shape

    def wide(n):
        return pl.BlockSpec((n, tile), lambda i: (0, i))

    edges = [pl.BlockSpec((BAND, tile), lambda i, lo=lo, hi=hi: (0, jnp.clip(i - lo, 0, hi - lo - 1))) for lo, hi in parts]
    return pl.pallas_call(
        functools.partial(conv_kernel, parts),
        grid=(hidden // tile,),
        in_specs=[wide(rows)] + edges + edges + [wide(9), wide(1)],
        out_specs=wide(rows),
        out_shape=jax.ShapeDtypeStruct((rows, hidden), jnp.bfloat16),
        scratch_shapes=[pltpu.VMEM((GRIDW + 16, LANES), jnp.float32)] * 2,
        compiler_params=pltpu.CompilerParams(vmem_limit_bytes=24 << 20),
        cost_estimate=pl.CostEstimate(flops=60 * rows * hidden, bytes_accessed=4 * rows * hidden, transcendentals=0),
    )(pre, *befores, *afters, taps, bias[None])


def local(tokens, w_in, b_in, dw_kernel, dw_bias, w_out, b_out):
    nt, nc = lax.axis_size("tok"), lax.axis_size("ch")
    nz, nx, ny = nt, nc // nt, nt // CORES
    t, c = lax.axis_index("tok"), lax.axis_index("ch")
    z, x = c // nx, c % nx
    y, core = t // CORES, t % CORES
    rows, width = tokens.shape
    depth, hidden = w_in.shape
    tile = hidden // TILES
    parts = [(0, TILES - 1), (TILES - 1, TILES)]
    half = rows // 2

    def zshift(k):
        return [(i, (i + k * nx) % nc) for i in range(nc)]

    def xshift(k):
        return [(i, i // nx * nx + (i + k) % nx) for i in range(nc)]

    def yshift(k):
        return [(i, (i + CORES * k) % nt) for i in range(nt)]

    swap = [(i, i ^ 1) for i in range(nt)]

    def owner(k, other):
        return (y + ny - k) % ny * CORES + (1 - core if other else core)

    toks, places, across = [], [], []
    for s in range(nz):
        if s == 0:
            held = [tokens]
        elif s == 1:
            held = [lax.ppermute(tokens, "ch", zshift(1))]
        else:
            held = held if len(held) == 2 else [held[0][:half], held[0][half:]]
            held = [lax.ppermute(held[h], "ch", zshift(1)) for h in range(2)]
        across.append({})
        for h, block in enumerate(held):
            toks.append(block)
            places.append((h * half, s, 0))
            for k in range(1, nx):
                if s == nz - 1 and h == 1:
                    got = lax.ppermute(across[s - 1][h, k], "ch", zshift(1))
                else:
                    got = lax.ppermute(block, "ch", xshift(k))
                across[s][h, k] = got
                toks.append(got)
                places.append((h * half, s, k))

    starts = [(x + nx - k) % nx * width for k in range(nx)]
    starts += [(z + nz - owner(k, other)) % nz for k in range(ny) for other in (0, 1)]
    starts = jnp.stack(starts).astype(jnp.int32)
    partner = lax.ppermute(w_in, "tok", swap)
    pieces_in = []
    for n in range(TILES):
        row = []
        for k in range(1, ny):
            mine = lax.ppermute(w_in[:, n * tile:(n + 1) * tile], "tok", yshift(k))
            row += [mine, lax.ppermute(mine, "tok", swap)]
        pieces_in.append(row)
    up = [(i, i + 1) for i in range(nt - 1)]
    down = [(i + 1, i) for i in range(nt - 1)]
    pre, befores, afters = [], [], []
    for lo, hi in parts:
        weights, homes = [w_in, partner], []
        for n in range(lo, hi):
            homes.append([(0, n * tile), (1, n * tile)] + [(len(weights) + i, 0) for i in range(nt - 2)])
            weights += pieces_in[n]
        out, first, final = project(starts, b_in, toks, places, weights, homes, lo, pre, rows, depth, tile, nz)
        pre = [out]
        afters.append(lax.ppermute(first, "tok", down))
        befores.append(lax.ppermute(final, "tok", up))
    act = convolve(pre[0], befores, afters, dw_kernel, dw_bias, tile, parts)

    pieces = max(1, width // LANES)
    cols = width // pieces
    partner_out = lax.ppermute(w_out, "tok", swap)
    outs = []
    behind = None
    for q in range(pieces):

        def cut_of(array):
            return [lax.dynamic_slice_in_dim(array, (x + k) % nx * width + q * cols, cols, 1) for k in range(nx)]

        order = list(range(1, nx)) + [0]
        own = cut_of(w_out)
        joint = jnp.concatenate([own[k] for k in order], axis=1)
        theirs = cut_of(partner_out)
        near = [joint, jnp.concatenate([theirs[k] for k in order], axis=1)]
        near = [jnp.dot(act, b, preferred_element_type=jnp.float32).astype(jnp.bfloat16) for b in near]
        apart = q in (0, pieces - 1)
        groups = [[k] for k in order] if apart else [order]
        far = {}
        for group in groups:
            block = own[group[0]] if apart else joint
            for j in range(1, ny):
                mine = lax.ppermute(block, "tok", yshift(j))
                pair = lax.ppermute(mine, "tok", swap)
                dots = [jnp.dot(act, b, preferred_element_type=jnp.float32).astype(jnp.bfloat16) for b in (mine, pair)]
                for i, k in enumerate(group):
                    far.setdefault(k, [])
                    far[k] += [d[:, i * cols:(i + 1) * cols] for d in dots]

        def shares(k, cut):
            i = order.index(k)
            return jnp.concatenate([d[cut, i * cols:(i + 1) * cols] for d in near] + [d[cut] for d in far[k]], axis=1)

        step = rows // SPLITS
        bands = []
        for h in range(SPLITS):
            cut = slice(h * step, (h + 1) * step)
            depth_first = h == 1 and q == 0
            if depth_first:
                totals = [shares(k, cut) for k in range(nx)]
            else:
                arrived = [lax.ppermute(shares(k, cut), "ch", xshift(k)) for k in range(1, nx)]
                if behind is not None:
                    arrived, _ = lax.optimization_barrier((arrived, behind))
                total = shares(0, cut).astype(jnp.float32)
                for got in arrived:
                    total = total + got.astype(jnp.float32)
                totals = [total]

            def term(goal):
                at = (y + ny - goal // CORES) % ny * CORES + (goal + core) % CORES
                return jnp.concatenate([lax.dynamic_slice_in_dim(v, at * cols, cols, 1) for v in totals], axis=1)

            live = {j: term(z ^ j) for j in range(nz)}
            span = live[0].shape[1]
            bit = 1
            while bit < nz:
                away = [j for j in live if j & bit]
                packed = jnp.concatenate([live.pop(j).astype(jnp.bfloat16) for j in away], axis=1)
                if bit == 1 and not depth_first:
                    behind = packed
                got = lax.ppermute(packed, "ch", [(i, (i // nx ^ bit) * nx + i % nx) for i in range(nc)])
                for i, j in enumerate(away):
                    more = got[:, i * span:(i + 1) * span].astype(jnp.float32)
                    live[j ^ bit] = live[j ^ bit].astype(jnp.float32) + more
                bit *= 2
            if depth_first:
                mine = live[0][:, :cols]
                for k in range(1, nx):
                    away = live[0][:, k * cols:(k + 1) * cols].astype(jnp.bfloat16)
                    mine = mine + lax.ppermute(away, "ch", xshift(k)).astype(jnp.float32)
                live[0] = mine
            bands.append(live[0])
        outs.append(jnp.concatenate(bands, axis=0))
    return (jnp.concatenate(outs, axis=1) + b_out).astype(jnp.bfloat16)


def solution(mesh):
    in_specs = (
        P("tok", "ch"),
        P("tok", "ch"),
        P("ch"),
        P(None, "ch"),
        P("ch"),
        P("ch", "tok"),
        P("ch"),
    )
    return jax.shard_map(local, mesh=mesh, in_specs=in_specs, out_specs=P("tok", "ch"), check_vma=False)
```

```python
import functools

import jax
import jax.numpy as jnp
from jax import lax
from jax.experimental import pallas as pl
from jax.experimental.pallas import tpu as pltpu
from jax.sharding import PartitionSpec as P

IMAGES = 2
GRIDW = 64
BAND = IMAGES * GRIDW
CORES = 2
LANES = 128
TILES = 4
SPLITS = 2
MM_VMEM = 60 << 20
MM_ROWS = 512


def mm_kernel(places, homes, base, start_ref, bias_ref, *refs):
    many = max(i for tile_homes in homes for i, _ in tile_homes) + 1
    toks, weights = refs[:len(places)], refs[len(places):len(places) + many]
    out, first, final, tok, held, stage, acc, tsem, wsem, osem = refs[-10:]
    nz, rows, _ = tok.shape
    _, tile = held.shape[2:]
    nx = start_ref.shape[0] - nz

    def tok_copy(i):
        row, s, k = places[i]
        n, width = toks[i].shape
        col = pl.multiple_of(start_ref[k], width)
        return pltpu.make_async_copy(toks[i], tok.at[s, pl.ds(row, n), pl.ds(col, width)], tsem.at[i])

    def weight_copy(t, r):
        ref, col = homes[t][r]
        slot = start_ref[nx + r]
        return pltpu.make_async_copy(weights[ref].at[:, pl.ds(col, tile)], held.at[t % 2, slot], wsem.at[t % 2, slot])

    def weight_wait(t, s):
        pltpu.make_async_copy(weights[0].at[:, pl.ds(0, tile)], held.at[t % 2, s], wsem.at[t % 2, s]).wait()

    def out_copies(t):
        cols = pl.ds(t * tile, tile)
        kept = stage.at[t % 2]
        return [
            pltpu.make_async_copy(kept, out.at[:, pl.ds((base + t) * tile, tile)], osem.at[t % 2, 0]),
            pltpu.make_async_copy(kept.at[pl.ds(0, BAND)], first.at[:, cols], osem.at[t % 2, 1]),
            pltpu.make_async_copy(kept.at[pl.ds(rows - BAND, BAND)], final.at[:, cols], osem.at[t % 2, 2]),
        ]

    tiles = len(homes)
    step = min(MM_ROWS, rows)
    by_slot = [[i for i in range(len(places)) if places[i][1] == s] for s in range(nz)]
    for i in by_slot[0]:
        tok_copy(i).start()
    for r in range(nz):
        weight_copy(0, r).start()
    for s in range(1, nz):
        for i in by_slot[s]:
            tok_copy(i).start()
    for t in range(tiles):
        if t + 1 < tiles:
            for r in range(nz):
                weight_copy(t + 1, r).start()
        if t >= 2:
            for copy in out_copies(t - 2):
                copy.wait()
        for group in ([[s] for s in range(nz)] if t == 0 else [list(range(nz))]):
            for s in group:
                if t == 0:
                    for i in by_slot[s]:
                        tok_copy(i).wait()
                weight_wait(t, s)

            def body(m, _, group=group, t=t):
                at = pl.ds(pl.multiple_of(m * step, step), step)
                if group[0] == 0:
                    total = bias_ref[:, (base + t) * tile:(base + t + 1) * tile] + jnp.zeros((step, tile), jnp.float32)
                else:
                    total = acc[at, :]
                for s in group:
                    total = total + jnp.dot(tok[s, at, :], held[t % 2, s], preferred_element_type=jnp.float32)
                if group[-1] == nz - 1:
                    stage[t % 2, at, :] = total.astype(stage.dtype)
                else:
                    acc[at, :] = total
                return 0

            lax.fori_loop(0, rows // step, body, 0)
        for copy in out_copies(t):
            copy.start()
    for t in range(max(0, tiles - 2), tiles):
        for copy in out_copies(t):
            copy.wait()


def project(starts, bias, toks, places, weights, homes, base, old, rows, depth, tile, nz):
    part = tile * len(homes)
    anywhere = pl.BlockSpec(memory_space=pl.ANY)
    return pl.pallas_call(
        functools.partial(mm_kernel, places, homes, base),
        in_specs=[pl.BlockSpec(memory_space=pltpu.SMEM), pl.BlockSpec(memory_space=pltpu.VMEM)]
        + [anywhere] * (len(toks) + len(weights) + len(old)),
        out_specs=[anywhere] * 3,
        out_shape=[jax.ShapeDtypeStruct(dims, jnp.bfloat16) for dims in ((rows, bias.shape[0]), (BAND, part), (BAND, part))],
        input_output_aliases={2 + len(toks) + len(weights) + i: i for i in range(len(old))},
        scratch_shapes=[
            pltpu.VMEM((nz, rows, depth), jnp.bfloat16),
            pltpu.VMEM((2, nz, depth, tile), jnp.bfloat16),
            pltpu.VMEM((2, rows, tile), jnp.bfloat16),
            pltpu.VMEM((rows, tile), jnp.float32),
            pltpu.SemaphoreType.DMA((len(toks),)),
            pltpu.SemaphoreType.DMA((2, nz)),
            pltpu.SemaphoreType.DMA((2, 3)),
        ],
        compiler_params=pltpu.CompilerParams(vmem_limit_bytes=MM_VMEM),
        cost_estimate=pl.CostEstimate(flops=2 * rows * nz * depth * part, bytes_accessed=2 * nz * depth * (rows + part), transcendentals=0),
    )(starts, bias[None], *toks, *weights, *old)


def conv_kernel(parts, pre_ref, *refs):
    n = len(parts)
    taps_ref, bias_ref, out_ref, left, right, above, below = refs[2 * n:]
    for f, (lo, hi) in enumerate(parts):

        @pl.when((pl.program_id(0) >= lo) & (pl.program_id(0) < hi))
        def _(f=f):
            above[...] = refs[f][...]
            below[...] = refs[n + f][...]

    conv_tile(pre_ref, above, below, taps_ref, bias_ref, out_ref, left, right)


def conv_tile(pre_ref, before_ref, after_ref, taps_ref, bias_ref, out_ref, left, right):
    rows, tile = out_ref.shape
    height = rows // BAND

    def body(n, _):
        lanes = pl.ds(pl.multiple_of(n // IMAGES * LANES, LANES), LANES)
        first = n % IMAGES * GRIDW
        taps = [taps_ref[i:i + 1, lanes] for i in range(9)]
        bias = bias_ref[:, lanes]
        left[7:8] = jnp.zeros((1, LANES), jnp.float32)
        right[GRIDW:GRIDW + 1] = jnp.zeros((1, LANES), jnp.float32)

        def row(h):
            ref, base = pre_ref, h * BAND
            if h < 0:
                ref, base = before_ref, 0
            if h >= height:
                ref, base = after_ref, 0
            at = pl.ds(pl.multiple_of(first + base, GRIDW), GRIDW)
            return ref[at, lanes].astype(jnp.float32)

        above, here = row(-1), row(0)
        for h in range(height):
            below = row(h + 1)
            left[8:8 + GRIDW] = above * taps[0] + here * taps[3] + below * taps[6]
            right[0:GRIDW] = above * taps[2] + here * taps[5] + below * taps[8]
            conv = bias + (above * taps[1] + here * taps[4] + below * taps[7])
            conv = conv + left[7:7 + GRIDW] + right[1:1 + GRIDW]
            act = 0.5 * conv * (1.0 + lax.erf(conv * 0.5 ** 0.5))
            at = pl.ds(pl.multiple_of(first + h * BAND, GRIDW), GRIDW)
            out_ref[at, lanes] = act.astype(out_ref.dtype)
            above, here = here, below
        return 0

    lax.fori_loop(0, IMAGES * (tile // LANES), body, 0)


def convolve(pre, befores, afters, taps, bias, tile, parts):
    rows, hidden = pre.shape

    def wide(n):
        return pl.BlockSpec((n, tile), lambda i: (0, i))

    edges = [pl.BlockSpec((BAND, tile), lambda i, lo=lo, hi=hi: (0, jnp.clip(i - lo, 0, hi - lo - 1))) for lo, hi in parts]
    return pl.pallas_call(
        functools.partial(conv_kernel, parts),
        grid=(hidden // tile,),
        in_specs=[wide(rows)] + edges + edges + [wide(9), wide(1)],
        out_specs=wide(rows),
        out_shape=jax.ShapeDtypeStruct((rows, hidden), jnp.bfloat16),
        scratch_shapes=[pltpu.VMEM((GRIDW + 16, LANES), jnp.float32)] * 2 + [pltpu.VMEM((BAND, tile), jnp.bfloat16)] * 2,
        compiler_params=pltpu.CompilerParams(vmem_limit_bytes=24 << 20),
        cost_estimate=pl.CostEstimate(flops=60 * rows * hidden, bytes_accessed=4 * rows * hidden, transcendentals=0),
    )(pre, *befores, *afters, taps, bias[None])


def local(tokens, w_in, b_in, dw_kernel, dw_bias, w_out, b_out):
    nt, nc = lax.axis_size("tok"), lax.axis_size("ch")
    nz, nx, ny = nt, nc // nt, nt // CORES
    t, c = lax.axis_index("tok"), lax.axis_index("ch")
    z, x = c // nx, c % nx
    y, core = t // CORES, t % CORES
    rows, width = tokens.shape
    depth, hidden = w_in.shape
    tile = hidden // TILES
    parts = [(0, TILES - 1), (TILES - 1, TILES)]
    half = rows // 2

    def zshift(k):
        return [(i, (i + k * nx) % nc) for i in range(nc)]

    def xshift(k):
        return [(i, i // nx * nx + (i + k) % nx) for i in range(nc)]

    def yshift(k):
        return [(i, (i + CORES * k) % nt) for i in range(nt)]

    swap = [(i, i ^ 1) for i in range(nt)]

    def owner(k, other):
        return (y + ny - k) % ny * CORES + (1 - core if other else core)

    toks, places, across = [], [], []
    for s in range(nz):
        if s == 0:
            held = [tokens]
        elif s == 1:
            held = [lax.ppermute(tokens, "ch", zshift(1))]
        else:
            held = held if len(held) == 2 else [held[0][:half], held[0][half:]]
            held = [lax.ppermute(held[h], "ch", zshift(1)) for h in range(2)]
        across.append({})
        for h, block in enumerate(held):
            toks.append(block)
            places.append((h * half, s, 0))
            for k in range(1, nx):
                if s == nz - 1 and h == 1:
                    got = lax.ppermute(across[s - 1][h, k], "ch", zshift(1))
                else:
                    got = lax.ppermute(block, "ch", xshift(k))
                across[s][h, k] = got
                toks.append(got)
                places.append((h * half, s, k))

    starts = [(x + nx - k) % nx * width for k in range(nx)]
    starts += [(z + nz - owner(k, other)) % nz for k in range(ny) for other in (0, 1)]
    starts = jnp.stack(starts).astype(jnp.int32)
    partner = lax.ppermute(w_in, "tok", swap)
    pieces_in = []
    for n in range(TILES):
        row = []
        for k in range(1, ny):
            mine = lax.ppermute(w_in[:, n * tile:(n + 1) * tile], "tok", yshift(k))
            row += [mine, lax.ppermute(mine, "tok", swap)]
        pieces_in.append(row)
    up = [(i, i + 1) for i in range(nt - 1)]
    down = [(i + 1, i) for i in range(nt - 1)]
    pre, befores, afters = [], [], []
    for lo, hi in parts:
        weights, homes = [w_in, partner], []
        for n in range(lo, hi):
            homes.append([(0, n * tile), (1, n * tile)] + [(len(weights) + i, 0) for i in range(nt - 2)])
            weights += pieces_in[n]
        out, first, final = project(starts, b_in, toks, places, weights, homes, lo, pre, rows, depth, tile, nz)
        pre = [out]
        afters.append(lax.ppermute(first, "tok", down))
        befores.append(lax.ppermute(final, "tok", up))
    act = convolve(pre[0], befores, afters, dw_kernel, dw_bias, tile, parts)

    pieces = max(1, width // LANES)
    cols = width // pieces
    partner_out = lax.ppermute(w_out, "tok", swap)
    outs = []
    behind = None
    for q in range(pieces):

        def cut_of(array):
            return [lax.dynamic_slice_in_dim(array, (x + k) % nx * width + q * cols, cols, 1) for k in range(nx)]

        order = list(range(1, nx)) + [0]
        own = cut_of(w_out)
        joint = jnp.concatenate([own[k] for k in order], axis=1)
        theirs = cut_of(partner_out)
        near = [joint, jnp.concatenate([theirs[k] for k in order], axis=1)]
        near = [jnp.dot(act, b, preferred_element_type=jnp.float32).astype(jnp.bfloat16) for b in near]
        apart = q == 0
        groups = [[k] for k in order] if apart else [order]
        far = {}
        for group in groups:
            block = own[group[0]] if apart else joint
            for j in range(1, ny):
                mine = lax.ppermute(block, "tok", yshift(j))
                pair = lax.ppermute(mine, "tok", swap)
                dots = [jnp.dot(act, b, preferred_element_type=jnp.float32).astype(jnp.bfloat16) for b in (mine, pair)]
                for i, k in enumerate(group):
                    far.setdefault(k, [])
                    far[k] += [d[:, i * cols:(i + 1) * cols] for d in dots]

        def shares(k, cut):
            i = order.index(k)
            return jnp.concatenate([d[cut, i * cols:(i + 1) * cols] for d in near] + [d[cut] for d in far[k]], axis=1)

        step = rows // SPLITS
        bands = []
        for h in range(SPLITS):
            cut = slice(h * step, (h + 1) * step)
            depth_first = h == 1 and q == 0
            if depth_first:
                totals = [shares(k, cut) for k in range(nx)]
            else:
                arrived = [lax.ppermute(shares(k, cut), "ch", xshift(k)) for k in range(1, nx)]
                if behind is not None:
                    arrived, _ = lax.optimization_barrier((arrived, behind))
                total = shares(0, cut).astype(jnp.float32)
                for got in arrived:
                    total = total + got.astype(jnp.float32)
                totals = [total]

            def term(goal):
                at = (y + ny - goal // CORES) % ny * CORES + (goal + core) % CORES
                return jnp.concatenate([lax.dynamic_slice_in_dim(v, at * cols, cols, 1) for v in totals], axis=1)

            live = {j: term(z ^ j) for j in range(nz)}
            span = live[0].shape[1]
            bit = 1
            while bit < nz:
                away = [j for j in live if j & bit]
                packed = jnp.concatenate([live.pop(j).astype(jnp.bfloat16) for j in away], axis=1)
                if bit == 1 and not depth_first:
                    behind = packed
                got = lax.ppermute(packed, "ch", [(i, (i // nx ^ bit) * nx + i % nx) for i in range(nc)])
                for i, j in enumerate(away):
                    more = got[:, i * span:(i + 1) * span].astype(jnp.float32)
                    live[j ^ bit] = live[j ^ bit].astype(jnp.float32) + more
                bit *= 2
            if depth_first:
                mine = live[0][:, :cols]
                for k in range(1, nx):
                    away = live[0][:, k * cols:(k + 1) * cols].astype(jnp.bfloat16)
                    mine = mine + lax.ppermute(away, "ch", xshift(k)).astype(jnp.float32)
                live[0] = mine
            bands.append(live[0])
        outs.append(jnp.concatenate(bands, axis=0))
    return (jnp.concatenate(outs, axis=1) + b_out).astype(jnp.bfloat16)


def solution(mesh):
    in_specs = (
        P("tok", "ch"),
        P("tok", "ch"),
        P("ch"),
        P(None, "ch"),
        P("ch"),
        P("ch", "tok"),
        P("ch"),
    )
    return jax.shard_map(local, mesh=mesh, in_specs=in_specs, out_specs=P("tok", "ch"), check_vma=False)
```
